256 devices in a mesh: blk: 16 (over z, x_hi), wide: 16 (over x_lo, y, core).
Axes of the slice: x: 4 (x_hi: 2, x_lo: 2; x = x_hi * 2 + x_lo), y: 4, z: 8, core: 2. Of those that a mesh axis runs over, the one named last changes fastest.
Arguments:
- features: bfloat16 [32768, 512], P(('blk', 'wide')), may hold values from -6 to 6
- w_msg: bfloat16 [512, 512], replicated, may hold values from -0.25 to 0.25
- w_self: bfloat16 [512, 512], replicated, may hold values from -0.25 to 0.25
- block_index: int32 [16, 16, 16, 4], P('blk', 'wide'), may hold values from 0 to 15, as said below
- block_count: int32 [16, 16, 16], P('blk', 'wide'), may hold values from 1 to 4
- blocks: bfloat16 [16, 16, 16, 4, 128, 128], P('blk', 'wide'), may hold values from -6 to 6
- cotangent: bfloat16 [32768, 512], P(('blk', 'wide')), may hold values from -6 to 6
Outputs:
- layer_out: bfloat16 [32768, 512], P(('blk', 'wide'))
- grad_x: bfloat16 [32768, 512], P(('blk', 'wide'))
- grad_msg_w: float32 [512, 512], replicated
- grad_self_w: float32 [512, 512], replicated
The draws below stay inside these ranges and needn't reach their ends.
Inputs may be any that keep to these rules, and one draw needn't show every extreme that they name: `block_index`: within one destination tile the 4 slots name distinct source tiles.
All inputs are finite; a program needn't handle non-finite values.
Results may differ from the reference program's by a relative error of at most 0.023.
Values may be sent and summed in bfloat16 or wider, within the bound.
A program may use at most 64 MiB of HBM per device.

```python
import jax
import jax.numpy as jnp
from jax import lax

F = 512
TB = 128
K = 4
TILE_DEV = 1
DST_TILES = 16
SRC_TILES = 16
NODES = 32768
N_BLK = 16
N_WIDE = 16


def draw_block_index(key, part):
    scores = jax.random.randint(key, (N_BLK, N_WIDE, DST_TILES, SRC_TILES), 0, 65536)
    scores = scores * SRC_TILES + jnp.arange(SRC_TILES, dtype=jnp.int32)
    _, chosen = lax.top_k(scores, K)
    return chosen.astype(jnp.int32)


def draw_block_count(key, part):
    counts = jax.random.randint(key, (N_BLK * N_WIDE * DST_TILES,), 1, K + 1)
    spot_high = jax.random.randint(jax.random.fold_in(key, 1), (), 0, N_BLK * N_WIDE * DST_TILES)
    spot_low = (spot_high + 1 + jax.random.randint(jax.random.fold_in(key, 2), (), 0, N_BLK * N_WIDE * DST_TILES - 1)) % (N_BLK * N_WIDE * DST_TILES)
    counts = counts.at[spot_high].set(K)
    counts = counts.at[spot_low].set(1)
    return counts.reshape(N_BLK, N_WIDE, DST_TILES).astype(jnp.int32)


def with_spikes(entries, rng, source, target, parts, factor):
    owner, partner = [(jnp.arange(entries.shape[axis_at]) // (entries.shape[axis_at] // parts)).reshape([-1 if axis == axis_at else 1 for axis in range(entries.ndim)]) for axis_at in (source, target)]
    chosen = jax.random.permutation(rng, parts)[partner]
    strong = (owner == chosen) | (owner == (partner + parts // 2) % parts)
    return jnp.where(strong, factor * entries, entries)


def steps_of(key, dims, shards, smallest, top_value):
    def one(position, blocks):
        draws = jax.random.uniform(jax.random.fold_in(jax.random.fold_in(key, 6), position), (blocks,), jnp.float32, smallest / len(shards), top_value / len(shards))
        return jnp.repeat(jnp.exp(draws), dims[position] // blocks).reshape((-1,) + (1,) * (len(dims) - position - 1))

    factor_of = one(*shards[0])
    for cut in shards[1:]:
        factor_of = factor_of * one(*cut)
    return factor_of


def normal_values(key, extent, spread, reach, pieces=(), kind=jnp.bfloat16):
    array = spread * jax.random.normal(key, extent, jnp.float32)
    if pieces:
        array = array * steps_of(key, extent, pieces, -0.22, 0.18)
    return jnp.clip(array, -reach, reach).astype(kind)


def noise_with(key, shape, deviation, most, pieces, heavy, held_as=jnp.bfloat16):
    drawn = deviation * jax.random.normal(key, shape, jnp.float32)
    if pieces:
        drawn = drawn * steps_of(key, shape, pieces, -0.22, 0.18)
    return jnp.clip(with_spikes(drawn, jax.random.fold_in(key, 3), *heavy), -most, most).astype(held_as)


def setup_inputs(seed: int = 0) -> dict:
    streams_of = jax.random.split(jax.random.key(seed), 8)
    features = normal_values(streams_of[0], (NODES, F), 1.0, 6.0, ((0, 256),))
    w_msg = normal_values(streams_of[1], (F, F), F ** -0.5, 0.25)
    w_self = normal_values(streams_of[2], (F, F), F ** -0.5, 0.25)
    block_index = draw_block_index(jax.random.fold_in(streams_of[7], 71), 0)
    block_count = draw_block_count(jax.random.fold_in(streams_of[7], 71), 0)
    blocks = noise_with(streams_of[5], (N_BLK, N_WIDE, DST_TILES, K, TB, TB), 1.0, 6.0, ((0, 16), (1, 16)), (1, 2, 16, 2.0))
    cotangent = normal_values(streams_of[6], (NODES, F), 1.0, 6.0, ((0, 256),))
    return {"features": features, "w_msg": w_msg, "w_self": w_self, "block_index": block_index, "block_count": block_count, "blocks": blocks, "cotangent": cotangent}


def reference(features, w_msg, w_self, block_index, block_count, blocks, cotangent):
    message = jnp.dot(features, w_msg, preferred_element_type=jnp.float32).astype(jnp.bfloat16)
    msg_tiles = message.reshape(N_BLK, N_WIDE, TILE_DEV, TB, F)
    live_slot = (jnp.arange(K, dtype=jnp.int32)[None, None, None, :] < block_count[..., None]).astype(jnp.float32)
    lane_ids = jnp.arange(N_WIDE, dtype=jnp.int32)[:, None, None]

    def forward_group(inputs):
        index_b, live_b, blk_b = inputs
        sources = msg_tiles[index_b // TILE_DEV, lane_ids, index_b % TILE_DEV].astype(jnp.float32)
        masked = blk_b.astype(jnp.float32) * live_b[..., None, None]
        aggregate = jnp.einsum('wtkij,wtkjf->tif', masked, sources).reshape(DST_TILES * TB, F)
        row_sq = lax.optimization_barrier(jnp.sum(jnp.square(blk_b.astype(jnp.float32)), axis=-1))
        squares = jnp.einsum('wtk,wtki->ti', live_b, row_sq).reshape(DST_TILES * TB)
        return (aggregate, squares)
    aggregate, squares = lax.map(forward_group, (block_index, live_slot, blocks))
    aggregate = aggregate.reshape(NODES, F)
    degree = 1.0 + jnp.sqrt(squares.reshape(NODES))[:, None]
    pre = aggregate / degree + jnp.dot(features, w_self, preferred_element_type=jnp.float32)
    layer_out = (features.astype(jnp.float32) + jax.nn.silu(pre)).astype(jnp.bfloat16)
    sigmoid_pre = jax.nn.sigmoid(pre)
    pre_grad = (cotangent.astype(jnp.float32) * sigmoid_pre * (1.0 + pre * (1.0 - sigmoid_pre))).astype(jnp.bfloat16)
    agg_grad = (pre_grad.astype(jnp.float32) / degree).astype(jnp.bfloat16)
    agg_groups = agg_grad.reshape(N_BLK, DST_TILES, TB, F)

    def backward_group(carried, inputs):
        index_b, live_b, blk_b, agg_b = inputs
        masked = blk_b.astype(jnp.float32) * live_b[..., None, None]
        contribution = jnp.einsum('wtkij,tif->wtkjf', masked, agg_b.astype(jnp.float32))
        carried = carried.at[index_b // TILE_DEV, lane_ids, index_b % TILE_DEV].add(contribution)
        return (carried, None)
    initial = jnp.zeros((N_BLK, N_WIDE, TILE_DEV, TB, F), jnp.float32)
    msg_grad, _ = lax.scan(backward_group, initial, (block_index, live_slot, blocks, agg_groups))
    msg_grad = msg_grad.reshape(NODES, F).astype(jnp.bfloat16)
    grad_x = (cotangent.astype(jnp.float32) + jnp.dot(pre_grad, w_self.T, preferred_element_type=jnp.float32) + jnp.dot(msg_grad, w_msg.T, preferred_element_type=jnp.float32)).astype(jnp.bfloat16)
    grad_msg_w = jnp.dot(features.T, msg_grad, preferred_element_type=jnp.float32)
    grad_self_w = jnp.dot(features.T, pre_grad, preferred_element_type=jnp.float32)
    return (layer_out, grad_x, grad_msg_w, grad_self_w)
```

```python
import functools

import jax
import jax.numpy as jnp
from jax import lax
from jax.experimental import pallas as pl
from jax.experimental.pallas import tpu as pltpu
from jax.sharding import PartitionSpec as P

MESH = pl.DeviceIdType.MESH
BF = jnp.bfloat16
F32 = jnp.float32
NZ, NXH, NXL, NY, NC = 8, 2, 2, 4, 2
TB, F, K, T = 128, 512, 4, 16
XY_PEERS = [(dxl, dy) for dxl in (1, 0) for dy in (2, 1, 3, 0) if (dxl, dy) != (0, 0)]


def dot(a, b):
    return jnp.dot(a, b, preferred_element_type=F32)


def dot_t(a, b):
    return lax.dot_general(a, b, (((1,), (1,)), ((), ())), preferred_element_type=F32)


def kernel(
    feat, w_msg_h, w_self_h, idx, cnt, blk_h, cot_h,
    lo_out, gx_out, gm_out, gs_out,
    xall, xt, dmat, dtm, blkv, blkt, acc, tacc, tb, wm, ws, ct, xs_self,
    sqs, sqr, sq2, sqin, b1s, b1r, b2s, b2r, g, pgv, pw,
    rsr, rsl, rrr, rrl, xsend, xrecv,
    mats, ecr, ehalf, exs, exr, ezr, eg, eg2,
    lsem, sx, rx, sr, rr, sl, rl, ssq, rsq, sb1, rb1, sb2, rb2, sc, rc_, sg, rg,
    sdr, rdr, sdl, rdl, sdx, rdx, sec, rec, sex, rex, sez, rez, sea, rea, seb, reb,
):
    bi = lax.axis_index("blk")
    wi = lax.axis_index("wide")
    z, xh = lax.div(bi, 2), lax.rem(bi, 2)
    xl, y, c = lax.div(wi, 8), lax.rem(lax.div(wi, 2), 4), lax.rem(wi, 2)
    zr = lambda d: lax.rem(z + (d + 8), 8)
    qme = xl * 4 + y

    def dev(dz=0, dxh=0, dxl=0, dy=0, dc=0):
        return (
            zr(dz) * 2 + lax.rem(xh + dxh, 2),
            lax.rem(xl + dxl, 2) * 8 + lax.rem(y + (dy + 4), 4) * 2 + lax.rem(c + dc, 2),
        )

    def rcopy(src, dst, ss, rs, device):
        return pltpu.make_async_remote_copy(
            src_ref=src, dst_ref=dst, send_sem=ss, recv_sem=rs, device_id=device, device_id_type=MESH
        )

    def plane(r):
        return dict(dxh=lax.div(r, 8), dxl=lax.rem(lax.div(r, 4), 2), dy=lax.rem(r, 4))

    def piece(r):
        o = plane(r)
        return (
            lax.rem(xh + o["dxh"], 2) * 8
            + lax.rem(xl + o["dxl"], 2) * 4
            + lax.rem(y + o["dy"], 4)
        )

    barrier = pltpu.get_barrier_semaphore()

    def greet(r, carry):
        pl.semaphore_signal(barrier, inc=1, device_id=dev(**plane(r)), device_id_type=MESH)
        return carry

    lax.fori_loop(1, 16, greet, 0)
    for d in range(1, 8):
        pl.semaphore_signal(barrier, inc=1, device_id=dev(dz=d), device_id_type=MESH)
    pl.semaphore_signal(barrier, inc=1, device_id=dev(dc=1), device_id_type=MESH)

    c_feat = pltpu.make_async_copy(feat, xall.at[bi], lsem.at[0])
    c_blk = pltpu.make_async_copy(blk_h, blkv, lsem.at[1])
    c_wm = pltpu.make_async_copy(w_msg_h, wm, lsem.at[2])
    c_ws = pltpu.make_async_copy(w_self_h, ws, lsem.at[3])
    c_ct = pltpu.make_async_copy(cot_h, ct, lsem.at[4])
    for cp in (c_feat, c_blk, c_wm, c_ws, c_ct):
        cp.start()
    c_feat.wait()
    pl.semaphore_wait(barrier, 23)

    bp = z * 2 + (1 - xh)
    ax = rcopy(xall.at[bi], xall.at[bi], sx.at[0], rx.at[0], dev(dxh=1))
    ax.start()

    def slot(zz, q):
        return zz * 2 + (xh if q == 0 else 1 - xh)

    def ring_r(q, d):
        s = slot(zr(-(d - 1)), q)
        ref = xall.at[s] if d < 4 else xall.at[s, pl.ds(0, 64)]
        i = q * 4 + d - 1
        return rcopy(ref, ref, sr.at[i], rr.at[i], dev(dz=1))

    def ring_l(q, d):
        s = slot(zr(d - 1), q)
        ref = xall.at[s] if d < 4 else xall.at[s, pl.ds(64, 64)]
        i = q * 4 + d - 1
        return rcopy(ref, ref, sl.at[i], rl.at[i], dev(dz=-1))

    ring_r(0, 1).start()
    ring_l(0, 1).start()

    def tile_of(r):
        return 2 * lax.rem(r, 8) + lax.rem(c + 1 + lax.div(r, 8), 2)

    def prepare(r, carry):
        t = tile_of(r)
        n = cnt[t]
        total = jnp.zeros((TB, TB), F32)
        for k in range(K):
            v = blkv[t, k].T
            blkt[t, k] = v
            vf = v.astype(F32)
            total += jnp.where(jnp.full((TB, TB), n, jnp.int32) > k, vf * vf, 0.0)
        row = jnp.sum(total, axis=0, keepdims=True)
        sqs[lax.div(r, 8), lax.rem(r, 8)] = jnp.broadcast_to(row, (8, TB))
        return carry

    c_blk.wait()
    lax.fori_loop(0, 8, prepare, 0)
    q1 = rcopy(sqs.at[0], sqr, ssq.at[0], rsq.at[0], dev(dc=1))
    q1.start()
    ax.wait_recv()
    ring_r(1, 1).start()
    ring_l(1, 1).start()
    lax.fori_loop(8, 16, prepare, 0)

    def densify(zz):
        def row(r, carry):
            t = tile_of(r)
            rel, q = lax.div(r, 8), lax.rem(r, 8)
            n = cnt[t]
            for xs in range(2):
                s = 2 * zz + xs
                kk = jnp.int32(0)
                live = jnp.int32(0)
                for k in range(K):
                    hit = jnp.logical_and(idx[t, k] == s, k < n)
                    kk = jnp.where(hit, k, kk)
                    live = jnp.where(hit, 1, live)
                m = jnp.full((TB, TB), live, jnp.int32) > 0
                v = blkv[t, kk].astype(F32)
                vt = blkt[t, kk].astype(F32)
                dmat[zz, rel, pl.ds(pl.multiple_of(q * TB, TB), TB), pl.ds(xs * TB, TB)] = jnp.where(
                    m, v, 0.0
                ).astype(BF)
                dtm[zz, pl.ds(xs * TB, TB), pl.ds(pl.multiple_of(r * TB, TB), TB)] = jnp.where(
                    m, vt, 0.0
                ).astype(BF)
            return carry

        lax.fori_loop(0, 16, row, 0)

    def messages(zz):
        xp = xall[pl.ds(2 * zz, 2)].reshape(2 * TB, F)
        xt[zz] = xp.T
        return dot(xp, wm[...]).astype(BF)

    def pair(zz, first=False):
        densify(zz)
        mp = messages(zz)
        for rel in range(2):
            for h in range(2):
                rows = pl.ds(h * 512, 512)
                new = dot(dmat[zz, rel, rows], mp)
                acc[rel, rows] = new if first else acc[rel, rows] + new

    c_wm.wait()
    pair(z, first=True)
    c_ws.wait()
    xs_self[...] = dot(xall[bi], ws[...])
    q1.wait_recv()
    sq2[...] = sqs[1] + sqr[...]

    def q_of(dxl, dy):
        return lax.rem(xl + dxl, 2) * 4 + lax.rem(y + dy, 4)

    def q2(i):
        dxl, dy = XY_PEERS[i]
        return rcopy(sq2.at[q_of(dxl, dy)], sqin.at[i], ssq.at[1 + i], rsq.at[1 + i], dev(dxl=dxl, dy=dy))

    for i in range(7):
        q2(i).start()

    for d in range(1, 4):
        for q in range(2):
            ring_r(q, d).wait_recv()
            ring_r(q, d + 1).start()
            ring_l(q, d).wait_recv()
            ring_l(q, d + 1).start()

        def both(j, carry, d=d):
            pair(lax.rem(z + 8 + (2 * j - 1) * d, 8))
            return carry

        lax.fori_loop(0, 2, both, 0)

    z4 = zr(4)
    densify(z4)
    sq = sq2[qme]
    for i in range(7):
        q2(i).wait_recv()
        sq = sq + sqin[i]
    deg = 1.0 + jnp.sqrt(jnp.broadcast_to(sq[0:1], (TB, TB)).T)
    deg = jnp.concatenate([deg] * 4, axis=1)
    for q in range(2):
        ring_r(q, 4).wait_recv()
        ring_l(q, 4).wait_recv()
    mp4 = messages(z4)

    def b1(h):
        part = pl.ds(pl.multiple_of(lax.rem(xl + 1 + h, 2) * 512, 512), 512)
        return part, rcopy(b1s.at[part], b1r.at[part], sb1.at[h], rb1.at[h], dev(dc=1))

    for h in range(2):
        part, cp = b1(h)
        b1s[part] = (acc[0, part] + dot(dmat[z4, 0, part], mp4)).astype(BF)
        cp.start()
    for h in range(2):
        part, cp = b1(h)
        acc[1, part] += dot(dmat[z4, 1, part], mp4)

    def b2(i):
        dxl, dy = XY_PEERS[i]
        return rcopy(b2s.at[i], b2r.at[i], sb2.at[i], rb2.at[i], dev(dxl=dxl, dy=dy))

    def rows_of(q):
        return pl.ds(pl.multiple_of(q * TB, TB), TB)

    for h in range(2):
        b1(h)[1].wait_recv()
        for i, (dxl, dy) in enumerate(XY_PEERS):
            if dxl == 1 - h:
                rows = rows_of(q_of(dxl, dy))
                b2s[i] = (acc[1, rows] + b1r[rows].astype(F32)).astype(BF)
                b2(i).start()
    agg = acc[1, rows_of(qme)] + b1r[rows_of(qme)].astype(F32)
    c_ct.wait()
    for i in range(7):
        b2(i).wait_recv()
        agg = agg + b2r[i].astype(F32)

    pre = agg / deg + xs_self[...]
    sig = jax.nn.sigmoid(pre)
    x = xall[bi].astype(F32)
    lo_out[...] = (x + pre * sig).astype(BF)
    ctf = ct[...].astype(F32)
    pg = (ctf * sig * (1.0 + pre * (1.0 - sig))).astype(BF)
    pgv[...] = pg
    g[1, qme] = (pg.astype(F32) / deg).astype(BF)

    def c1(i):
        dxl, dy = XY_PEERS[i]
        ref = g.at[1, qme]
        return rcopy(ref, ref, sc.at[i], rc_.at[i], dev(dxl=dxl, dy=dy))

    def c2(i):
        if i == 7:
            q = qme
        else:
            dxl, dy = XY_PEERS[i]
            q = q_of(dxl, 4 - dy)
        return rcopy(g.at[1, q], g.at[0, q], sg.at[i], rg.at[i], dev(dc=1))

    for i in range(7):
        c1(i).start()
    c2(7).start()

    def e_core(m):
        return rcopy(mats.at[m, 1 - c], ecr.at[m], sec.at[m], rec.at[m], dev(dc=1))

    def e_xy(m, r):
        return rcopy(exs.at[m, r], exr.at[m, r], sex.at[m, r], rex.at[m, r], dev(**plane(r)))

    def e_z(m, d):
        return rcopy(ezr.at[m, z], ezr.at[m, z], sez.at[m, d], rez.at[m, d], dev(dz=d))

    def e_ag(m, r):
        ref = eg.at[m, piece(0)]
        return rcopy(ref, ref, sea.at[m, r], rea.at[m, r], dev(**plane(r)))

    def e_last(m):
        return rcopy(eg.at[m], eg2.at[m], seb.at[m], reb.at[m], dev(dc=1))

    def e_stage2(m):
        e_core(m).wait_recv()

        def send(r, carry):
            rows = pl.ds(pl.multiple_of(piece(r) * 16, 16), 16)
            exs[m, r] = (mats[m, c, rows] + ecr[m, rows]).astype(BF)
            e_xy(m, r).start()
            return carry

        lax.fori_loop(1, 16, send, 0)
        rows = pl.ds(pl.multiple_of(piece(0) * 16, 16), 16)
        ehalf[m] = mats[m, c, rows] + ecr[m, rows]

    def e_stage3(m):
        def take(r, total):
            e_xy(m, r).wait_recv()
            return total + exr[m, r].astype(F32)

        ezr[m, z] = lax.fori_loop(1, 16, take, ehalf[m]).astype(BF)
        for d in range(1, 8):
            e_z(m, d).start()

    def e_stage4(m):
        for d in range(1, 8):
            e_z(m, d).wait_recv()
        total = ezr[m, 0].astype(F32)
        for d in range(1, 8):
            total = total + ezr[m, d].astype(F32)
        eg[m, piece(0)] = total.astype(BF)

        def send(r, carry):
            e_ag(m, r).start()
            return carry

        lax.fori_loop(1, 16, send, 0)

    def e_stage5(m):
        def take(r, carry):
            e_ag(m, r).wait_recv()
            return carry

        lax.fori_loop(1, 16, take, 0)
        e_last(m).start()

    def e_finish(m, out):
        out[pl.ds(pl.multiple_of(c * 256, 256), 256)] = eg[m].reshape(256, F).astype(F32)
        e_last(m).wait_recv()
        out[pl.ds(pl.multiple_of((1 - c) * 256, 256), 256)] = eg2[m].reshape(256, F).astype(F32)

    mats[0] = dot(xall[bi].T, pgv[...]).reshape(2, 256, F)
    e_core(0).start()
    pw[...] = ctf + dot_t(pgv[...], ws[...])

    for i in (3, 5, 6, 4, 1, 2, 0):
        c1(i).wait_recv()
        c2(i).start()
    e_stage2(0)

    def half_t(zz, carry):
        tacc[zz] = dot(dtm[zz, :, pl.ds(1024, 1024)], g[1].reshape(1024, F))
        return carry

    lax.fori_loop(0, 8, half_t, 0)
    for i in range(8):
        c2(i).wait_recv()

    def full_t(zz):
        v = tacc[zz] + dot(dtm[zz, :, pl.ds(0, 1024)], g[0].reshape(1024, F))
        tacc[zz] = v
        tb[zz] = v.astype(BF)

    def dr(k, h):
        i = (k - 1) * 2 + h
        if k == 1:
            src, dst = tb.at[z4, pl.ds(h * TB, 64)], rrr.at[0, pl.ds(h * TB, 64)]
        else:
            src, dst = rsr.at[k - 2, pl.ds(h * TB, TB)], rrr.at[k - 1, pl.ds(h * TB, TB)]
        return rcopy(src, dst, sdr.at[i], rdr.at[i], dev(dz=1))

    def dl(k, h):
        i = (k - 1) * 2 + h
        if k == 1:
            src, dst = tb.at[z4, pl.ds(h * TB + 64, 64)], rrl.at[0, pl.ds(h * TB + 64, 64)]
        else:
            src, dst = rsl.at[k - 2, pl.ds(h * TB, TB)], rrl.at[k - 1, pl.ds(h * TB, TB)]
        return rcopy(src, dst, sdl.at[i], rdl.at[i], dev(dz=-1))

    full_t(z4)
    for h in range(2):
        dr(1, h).start()
        dl(1, h).start()

    def others(j, carry):
        full_t(lax.rem(z + 5 + j, 8))
        return carry

    lax.fori_loop(0, 7, others, 0)

    def grad_m(zz, carry):
        new = dot(xt[zz], tb[zz]).reshape(2, 256, F)
        mats[1] = mats[1] + new
        return carry

    mats[1] = dot(xt[0], tb[0]).reshape(2, 256, F)
    lax.fori_loop(1, 8, grad_m, 0)
    e_core(1).start()

    def ring_step(k):
        for h in range(2):
            for copy, recv, send, zz, low in (
                (dr, rrr, rsr, zr(5 - k), 0),
                (dl, rrl, rsl, zr(k - 5), 64),
            ):
                copy(k - 1, h).wait_recv()
                if k == 2:
                    part, rest = pl.ds(h * TB + low, 64), pl.ds(h * TB + 64 - low, 64)
                    send[0, rest] = tb[zz, rest]
                else:
                    part = pl.ds(h * TB, TB)
                send[k - 2, part] = (tacc[zz, part] + recv[k - 2, part].astype(F32)).astype(BF)
                copy(k, h).start()

    ring_step(2)
    e_stage3(0)
    e_stage2(1)
    ring_step(3)
    e_stage4(0)
    ring_step(4)
    e_stage3(1)
    e_stage5(0)
    for h in range(2):
        dr(4, h).wait_recv()
        dl(4, h).wait_recv()
    dx = rcopy(xsend, xrecv, sdx.at[0], rdx.at[0], dev(dxh=1))
    far = pl.ds(pl.multiple_of((1 - xh) * TB, TB), TB)
    near = pl.ds(pl.multiple_of(xh * TB, TB), TB)
    xsend[...] = (tacc[z, far] + rrr[3, far].astype(F32) + rrl[3, far].astype(F32)).astype(BF)
    dx.start()
    own = tacc[z, near] + rrr[3, near].astype(F32) + rrl[3, near].astype(F32)
    e_stage4(1)
    dx.wait_recv()
    mg = (own + xrecv[...].astype(F32)).astype(BF)
    gx_out[...] = (pw[...] + dot_t(mg, wm[...])).astype(BF)
    e_finish(0, gs_out)
    e_stage5(1)
    e_finish(1, gm_out)

    ax.wait_send()
    for q in range(2):
        for d in range(1, 5):
            ring_r(q, d).wait_send()
            ring_l(q, d).wait_send()
    q1.wait_send()
    for h in range(2):
        b1(h)[1].wait_send()
    for i in range(7):
        q2(i).wait_send()
        b2(i).wait_send()
        c1(i).wait_send()
    for i in range(8):
        c2(i).wait_send()
    for k in range(1, 5):
        for h in range(2):
            dr(k, h).wait_send()
            dl(k, h).wait_send()
    dx.wait_send()
    for m in range(2):
        e_core(m).wait_send()

        def sent(r, carry, m=m):
            e_xy(m, r).wait_send()
            e_ag(m, r).wait_send()
            return carry

        lax.fori_loop(1, 16, sent, 0)
        for d in range(1, 8):
            e_z(m, d).wait_send()
        e_last(m).wait_send()


def shards(features, w_msg, w_self, block_index, block_count, blocks, cotangent):
    any_, smem, vmem = (pl.BlockSpec(memory_space=s) for s in (pl.ANY, pltpu.SMEM, pltpu.VMEM))
    V, D = pltpu.VMEM, pltpu.SemaphoreType.DMA
    scratch = [
        V((16, TB, F), BF),
        V((8, F, 2 * TB), BF),
        V((8, 2, 1024, 256), BF),
        V((8, 256, 2048), BF),
        V((T, K, TB, TB), BF),
        V((T, K, TB, TB), BF),
        V((2, 1024, F), F32),
        V((8, 256, F), F32),
        V((8, 256, F), BF),
        V((F, F), BF),
        V((F, F), BF),
        V((TB, F), BF),
        V((TB, F), F32),
        V((2, 8, 8, TB), F32),
        V((8, 8, TB), F32),
        V((8, 8, TB), F32),
        V((7, 8, TB), F32),
        V((1024, F), BF),
        V((1024, F), BF),
        V((7, TB, F), BF),
        V((7, TB, F), BF),
        V((2, 8, TB, F), BF),
        V((TB, F), BF),
        V((TB, F), F32),
        V((3, 256, F), BF),
        V((3, 256, F), BF),
        V((4, 256, F), BF),
        V((4, 256, F), BF),
        V((TB, F), BF),
        V((TB, F), BF),
        V((2, 2, 256, F), F32),
        V((2, 256, F), F32),
        V((2, 16, F), F32),
        V((2, 16, 16, F), BF),
        V((2, 16, 16, F), BF),
        V((2, 8, 16, F), BF),
        V((2, 16, 16, F), BF),
        V((2, 16, 16, F), BF),
        D((5,)),
        D((1,)), D((1,)),
        D((8,)), D((8,)), D((8,)), D((8,)),
        D((8,)), D((8,)),
        D((2,)), D((2,)), D((7,)), D((7,)),
        D((7,)), D((7,)), D((8,)), D((8,)),
        D((8,)), D((8,)), D((8,)), D((8,)),
        D((1,)), D((1,)),
        D((2,)), D((2,)), D((2, 16)), D((2, 16)), D((2, 8)), D((2, 8)),
        D((2, 16)), D((2, 16)), D((2,)), D((2,)),
    ]
    return pl.pallas_call(
        kernel,
        out_shape=(
            jax.ShapeDtypeStruct((TB, F), BF),
            jax.ShapeDtypeStruct((TB, F), BF),
            jax.ShapeDtypeStruct((F, F), F32),
            jax.ShapeDtypeStruct((F, F), F32),
        ),
        in_specs=[any_, any_, any_, smem, smem, any_, any_],
        out_specs=(vmem, vmem, vmem, vmem),
        scratch_shapes=scratch,
        compiler_params=pltpu.CompilerParams(
            collective_id=0, has_side_effects=True, vmem_limit_bytes=58 * 1024 * 1024
        ),
        name="layer",
    )(
        features,
        w_msg,
        w_self,
        block_index.reshape(T, K),
        block_count.reshape(T),
        blocks.reshape(T, K, TB, TB),
        cotangent,
    )


def solution(mesh):
    return jax.shard_map(
        shards,
        mesh=mesh,
        in_specs=(
            P(("blk", "wide"), None),
            P(),
            P(),
            P("blk", "wide", None, None),
            P("blk", "wide", None),
            P("blk", "wide", None, None, None, None),
            P(("blk", "wide"), None),
        ),
        out_specs=(P(("blk", "wide"), None), P(("blk", "wide"), None), P(), P()),
        check_vma=False,
    )
```

```python
import functools

import jax
import jax.numpy as jnp
from jax import lax
from jax.experimental import pallas as pl
from jax.experimental.pallas import tpu as pltpu
from jax.sharding import PartitionSpec as P

MESH = pl.DeviceIdType.MESH
BF = jnp.bfloat16
F32 = jnp.float32
NZ, NXH, NXL, NY, NC = 8, 2, 2, 4, 2
TB, F, H, K, T = 128, 512, 256, 4, 16
XY_PEERS = [(dxl, dy) for dxl in (1, 0) for dy in (2, 1, 3, 0) if (dxl, dy) != (0, 0)]


def dot(a, b):
    return jnp.dot(a, b, preferred_element_type=F32)


def dot_t(a, b):
    return lax.dot_general(a, b, (((1,), (1,)), ((), ())), preferred_element_type=F32)


def kernel(
    feat, w_msg_h, w_self_h, idx, cnt, blk_h, cot_h,
    outs, gw_out,
    xall, xot, dmat, dtm, blkv, blkt, acc, tacc, wm, ws, ct, xs_self,
    sqs, sqr, sq2, sqin, b1s, b1r, b2s, b2r, g, pgv, pw,
    fxs, fxr, n4, nsr, nsl, nrr, nrl, fsr, fsl, frr, frl, xsend, xrecv,
    mats, ecr, ehalf, ezs, ezr, epc, exs, exr, ezt, eg, eg2,
    lsem, sx, rx, sr, rr, sl, rl, ssq, rsq, sb1, rb1, sb2, rb2, sc, rc_, sg, rg,
    sdr, rdr, sdl, rdl, sdx, rdx, sec, rec, sex, rex, sez, rez, sea, rea, seb, reb,
):
    bi = lax.axis_index("blk")
    wi = lax.axis_index("wide")
    z, xh = lax.div(bi, 2), lax.rem(bi, 2)
    xl, y, c = lax.div(wi, 8), lax.rem(lax.div(wi, 2), 4), lax.rem(wi, 2)
    zr = lambda d: lax.rem(z + (d + 8), 8)
    qme = xl * 4 + y

    def dev(dz=0, dxh=0, dxl=0, dy=0, dc=0):
        return (
            zr(dz) * 2 + lax.rem(xh + dxh, 2),
            lax.rem(xl + dxl, 2) * 8 + lax.rem(y + (dy + 4), 4) * 2 + lax.rem(c + dc, 2),
        )

    def rcopy(src, dst, ss, rs, device):
        return pltpu.make_async_remote_copy(
            src_ref=src, dst_ref=dst, send_sem=ss, recv_sem=rs, device_id=device, device_id_type=MESH
        )

    def plane(r):
        return dict(dxh=lax.div(r, 8), dxl=lax.rem(lax.div(r, 4), 2), dy=lax.rem(r, 4))

    def piece(r):
        o = plane(r)
        return (
            lax.rem(xh + o["dxh"], 2) * 8
            + lax.rem(xl + o["dxl"], 2) * 4
            + lax.rem(y + o["dy"], 4)
        )

    barrier = pltpu.get_barrier_semaphore()

    def greet(r, carry):
        pl.semaphore_signal(barrier, inc=1, device_id=dev(**plane(r)), device_id_type=MESH)
        return carry

    lax.fori_loop(1, 16, greet, 0)
    for d in range(1, 8):
        pl.semaphore_signal(barrier, inc=1, device_id=dev(dz=d), device_id_type=MESH)
    pl.semaphore_signal(barrier, inc=1, device_id=dev(dc=1), device_id_type=MESH)

    c_feat = [
        pltpu.make_async_copy(feat.at[:, pl.ds(h * H, H)], xall.at[h, bi], lsem.at[5 * h])
        for h in range(2)
    ]
    c_blk = pltpu.make_async_copy(blk_h, blkv, lsem.at[1])
    c_wm = pltpu.make_async_copy(w_msg_h, wm, lsem.at[2])
    c_ws = pltpu.make_async_copy(w_self_h, ws, lsem.at[3])
    c_ct = pltpu.make_async_copy(cot_h, ct, lsem.at[4])
    for cp in (*c_feat, c_blk, c_wm, c_ws, c_ct):
        cp.start()
    for cp in c_feat:
        cp.wait()
    pl.semaphore_wait(barrier, 23)

    def slot(zz, q):
        return zz * 2 + (xh if q == 0 else 1 - xh)

    def ax(ch):
        ref = xall.at[ch, bi]
        return rcopy(ref, ref, sx.at[ch], rx.at[ch], dev(dxh=1))

    def ring(sign, q, d, ch):
        behind, places = (2, 2) if d == 4 else (d - 1, 1)
        ref = xall.at[ch, slot(zr(-sign * behind), q)]
        i = q * 8 + (d - 1) * 2 + ch if q == 0 else 8 + d - 1
        ss, rs = (sr, rr) if sign > 0 else (sl, rl)
        return rcopy(ref, ref, ss.at[i], rs.at[i], dev(dz=sign * places))

    def across(sign, d):
        ch = 1 if d < 4 else (0 if sign > 0 else 1)
        ref = xall.at[ch, slot(zr(-sign * d), 0)]
        i = 2 + (d - 1) * 2 + (0 if sign > 0 else 1)
        return rcopy(ref, ref, sx.at[i], rx.at[i], dev(dxh=1))

    for ch in range(2):
        ring(1, 0, 1, ch).start()
        ring(-1, 0, 1, ch).start()
        ax(ch).start()

    def tile_of(r):
        return 2 * lax.rem(r, 8) + lax.rem(c + 1 + lax.div(r, 8), 2)

    def prepare(r, carry):
        t = tile_of(r)
        n = cnt[t]
        total = jnp.zeros((TB, TB), F32)
        for k in range(K):
            v = blkv[t, k].T
            blkt[t, k] = v
            vf = v.astype(F32)
            total += jnp.where(jnp.full((TB, TB), n, jnp.int32) > k, vf * vf, 0.0)
        row = jnp.sum(total, axis=0, keepdims=True)
        sqs[lax.div(r, 8), lax.rem(r, 8)] = jnp.broadcast_to(row, (8, TB))
        return carry

    c_blk.wait()
    lax.fori_loop(0, 8, prepare, 0)
    q1 = rcopy(sqs.at[0], sqr, ssq.at[0], rsq.at[0], dev(dc=1))
    q1.start()
    ax(0).wait_recv()
    ring(1, 1, 1, 0).start()
    ring(-1, 1, 1, 0).start()
    lax.fori_loop(8, 16, prepare, 0)

    def densify(zz):
        def row(r, carry):
            t = tile_of(r)
            rel, q = lax.div(r, 8), lax.rem(r, 8)
            n = cnt[t]
            for xs in range(2):
                s = 2 * zz + xs
                kk = jnp.int32(0)
                live = jnp.int32(0)
                for k in range(K):
                    hit = jnp.logical_and(idx[k, t] == s, k < n)
                    kk = jnp.where(hit, k, kk)
                    live = jnp.where(hit, 1, live)
                m = jnp.full((TB, TB), live, jnp.int32) > 0
                v = blkv[t, kk].astype(F32)
                vt = blkt[t, kk].astype(F32)
                dmat[zz, rel, pl.ds(pl.multiple_of(q * TB, TB), TB), pl.ds(xs * TB, TB)] = jnp.where(
                    m, v, 0.0
                ).astype(BF)
                dtm[zz, pl.ds(xs * TB, TB), pl.ds(pl.multiple_of(r * TB, TB), TB)] = jnp.where(
                    m, vt, 0.0
                ).astype(BF)
            return carry

        lax.fori_loop(0, 16, row, 0)

    def panel(zz, h):
        return xall[h, pl.ds(2 * zz, 2)].reshape(2 * TB, H)

    def pair(zz, first=False):
        densify(zz)
        for h in range(2):
            xp = panel(zz, h)
            for rel in range(2):
                for part in range(2):
                    rows = pl.ds(part * 512, 512)
                    new = dot(dmat[zz, rel, rows], xp)
                    acc[h, rel, rows] = new if first else acc[h, rel, rows] + new

    def pairs(d):
        def one(j, carry):
            pair(lax.rem(z + 8 + (2 * j - 1) * d, 8))
            return carry

        lax.fori_loop(0, 2, one, 0)

    def forward(d):
        for sign in (1, -1):
            for ch in range(2):
                ring(sign, 0, d, ch).wait_recv()
                if d < 3:
                    ring(sign, 0, d + 1, ch).start()
                if d == 2 and ch == (0 if sign > 0 else 1):
                    ring(sign, 0, 4, ch).start()
                if ch == 1:
                    across(sign, d).start()
        for sign in (1, -1):
            ring(sign, 1, d, 0).wait_recv()
            if d < 3:
                ring(sign, 1, d + 1, 0).start()

    def q_of(dxl, dy):
        return lax.rem(xl + dxl, 2) * 4 + lax.rem(y + dy, 4)

    def q2(i):
        dxl, dy = XY_PEERS[i]
        return rcopy(sq2.at[q_of(dxl, dy)], sqin.at[i], ssq.at[1 + i], rsq.at[1 + i], dev(dxl=dxl, dy=dy))

    forward(1)
    ax(1).wait_recv()
    pair(z, first=True)
    q1.wait_recv()
    sq2[...] = sqs[1] + sqr[...]
    for i in range(7):
        q2(i).start()
    forward(2)
    for sign in (1, -1):
        across(sign, 1).wait_recv()
    pairs(1)
    forward(3)
    for sign in (1, -1):
        across(sign, 2).wait_recv()
    pairs(2)
    c_ws.wait()
    xs_self[...] = dot(xall[0, bi], ws[pl.ds(0, H)]) + dot(xall[1, bi], ws[pl.ds(H, H)])
    for h in range(2):
        xot[pl.ds(h * H, H)] = xall[h, bi].T
    for sign in (1, -1):
        ring(sign, 0, 4, 0 if sign > 0 else 1).wait_recv()
        across(sign, 4).start()
    for sign in (1, -1):
        across(sign, 3).wait_recv()
    pairs(3)
    z4 = zr(4)
    densify(z4)
    c_wm.wait()
    sq = sq2[qme]
    for i in range(7):
        q2(i).wait_recv()
        sq = sq + sqin[i]
    deg = 1.0 + jnp.sqrt(jnp.broadcast_to(sq[0:1], (TB, TB)).T)
    deg = jnp.concatenate([deg] * 2, axis=1)

    def b1(h, p):
        part = pl.ds(pl.multiple_of(lax.rem(xl + 1 + p, 2) * 512, 512), 512)
        i = 2 * h + p
        return part, rcopy(b1s.at[h, part], b1r.at[h, part], sb1.at[i], rb1.at[i], dev(dc=1))

    def b2(h, i):
        dxl, dy = XY_PEERS[i]
        j = 7 * h + i
        return rcopy(b2s.at[h, i], b2r.at[h, i], sb2.at[j], rb2.at[j], dev(dxl=dxl, dy=dy))

    def rows_of(q):
        return pl.ds(pl.multiple_of(q * TB, TB), TB)

    for h in range(2):
        across(1 if h == 0 else -1, 4).wait_recv()
        xp4 = panel(z4, h)
        for p in range(2):
            part, cp = b1(h, p)
            b1s[h, part] = (acc[h, 0, part] + dot(dmat[z4, 0, part], xp4)).astype(BF)
            cp.start()
        for p in range(2):
            part, cp = b1(h, p)
            acc[h, 1, part] += dot(dmat[z4, 1, part], xp4)
        for p in range(2):
            b1(h, p)[1].wait_recv()
            for i, (dxl, dy) in enumerate(XY_PEERS):
                if dxl == 1 - p:
                    rows = rows_of(q_of(dxl, dy))
                    b2s[h, i] = (acc[h, 1, rows] + b1r[h, rows].astype(F32)).astype(BF)
                    b2(h, i).start()
    c_ct.wait()
    agg = []
    for h in range(2):
        total = acc[h, 1, rows_of(qme)] + b1r[h, rows_of(qme)].astype(F32)
        for i in range(7):
            b2(h, i).wait_recv()
            total = total + b2r[h, i].astype(F32)
        agg.append(total)

    aggh = [v.astype(BF) for v in agg]
    aggl = [(v - hi.astype(F32)).astype(BF) for v, hi in zip(agg, aggh)]

    def c1(h, i):
        dxl, dy = XY_PEERS[i]
        ref = g.at[h, 1, qme]
        j = 7 * h + i
        return rcopy(ref, ref, sc.at[j], rc_.at[j], dev(dxl=dxl, dy=dy))

    def c2(h, i):
        if i == 7:
            q = qme
        else:
            dxl, dy = XY_PEERS[i]
            q = q_of(dxl, 4 - dy)
        j = 8 * h + i
        return rcopy(g.at[h, 1, q], g.at[h, 0, q], sg.at[j], rg.at[j], dev(dc=1))

    for h in range(2):
        cols = pl.ds(h * H, H)
        lin = xs_self[:, cols]
        new = sum(
            dot(v[f], wm[pl.ds(f * H, H), cols]) for v in (aggh, aggl) for f in range(2)
        )
        pre = new / deg + lin
        sig = jax.nn.sigmoid(pre)
        outs[0, :, cols] = (xall[h, bi].astype(F32) + pre * sig).astype(BF)
        ctf = ct[:, cols].astype(F32)
        pg = (ctf * sig * (1.0 + pre * (1.0 - sig))).astype(BF)
        pgv[:, cols] = pg
        g[h, 1, qme] = (pg.astype(F32) / deg).astype(BF)
        for i in range(7):
            c1(h, i).start()
        c2(h, 7).start()

    e_core = rcopy(mats.at[1 - c], ecr, sec.at[0], rec.at[0], dev(dc=1))
    e_last = rcopy(eg, eg2, seb.at[0], reb.at[0], dev(dc=1))

    def e_z(d):
        return rcopy(ezs.at[d], ezr.at[d], sez.at[d], rez.at[d], dev(dz=d))

    def e_xy(r):
        return rcopy(exs.at[r], exr.at[r], sex.at[r], rex.at[r], dev(**plane(r)))

    def e_back(d):
        return rcopy(ezt.at[z], ezt.at[z], sez.at[7 + d], rez.at[7 + d], dev(dz=d))

    def e_ag(r):
        ref = eg.at[piece(0)]
        return rcopy(ref, ref, sea.at[r], rea.at[r], dev(**plane(r)))

    def e_stage2():
        e_core.wait_recv()
        for d in (4, 3, 5, 2, 6, 1, 7, 0):
            rows = pl.ds(pl.multiple_of(zr(d) * 64, 64), 64)
            v = mats[c, rows] + ecr[rows]
            if d:
                ezs[d] = v.astype(BF)
                e_z(d).start()
            else:
                ehalf[...] = v

    def e_stage3():
        v = ehalf[...]
        for d in range(1, 8):
            e_z(d).wait_recv()
            v = v + ezr[d].astype(F32)
        for p in range(16):
            epc[p] = v[p // 4 * 16 : p // 4 * 16 + 16, p % 4 * TB : p % 4 * TB + TB]

        def send(r, carry):
            exs[r] = epc[piece(r)].astype(BF)
            e_xy(r).start()
            return carry

        lax.fori_loop(1, 16, send, 0)

    def e_stage4():
        def take(r, total):
            e_xy(r).wait_recv()
            return total + exr[r].astype(F32)

        ezt[z] = lax.fori_loop(1, 16, take, epc[piece(0)]).astype(BF)
        for d in range(1, 8):
            e_back(d).start()

    def e_stage5():
        for d in range(1, 8):
            e_back(d).wait_recv()
        eg[piece(0)] = ezt[...]

        def send(r, carry):
            e_ag(r).start()
            return carry

        lax.fori_loop(1, 16, send, 0)

    def e_stage6():
        def take(r, carry):
            e_ag(r).wait_recv()
            return carry

        lax.fori_loop(1, 16, take, 0)
        e_last.start()

    mats[0] = dot(xot[...], pgv[...])
    for f in range(2):
        aggt = aggh[f].T
        for h in range(2):
            mats[1, pl.ds(f * H, H), pl.ds(h * H, H)] = dot(aggt, g[h, 1, qme])
    e_core.start()
    pw[...] = ct[...].astype(F32) + dot_t(pgv[...], ws[...])

    def half_t(h, zz):
        tacc[h, zz] = dot(dtm[zz, :, pl.ds(1024, 1024)], g[h, 1].reshape(1024, H))

    def full_t(h, zz):
        tacc[h, zz] += dot(dtm[zz, :, pl.ds(0, 1024)], g[h, 0].reshape(1024, H))

    def rest(h, zz):
        half_t(h, zz)
        full_t(h, zz)

    near = pl.ds(pl.multiple_of(xh * TB, TB), TB)
    far = pl.ds(pl.multiple_of((1 - xh) * TB, TB), TB)

    def dx(h, d):
        ref_s, ref_r = fxs.at[h, zr(d)], fxr.at[h, zr(d)]
        i = d % 8 if h == 1 else 8
        return rcopy(ref_s, ref_r, sdx.at[i], rdx.at[i], dev(dxh=1))

    def send_x(h, d):
        fxs[h, zr(d)] = tacc[h, zr(d), far].astype(BF)
        dx(h, d).start()

    def sums(sign, k, h, is_far=False):
        if is_far:
            i = 8 + k - 2
            src, dst = (fsr, frr) if sign > 0 else (fsl, frl)
            src, dst = src.at[k - 2], dst.at[k - 2]
        else:
            i = (k - 1) * 2 + h
            src, dst = (nsr, nrr) if sign > 0 else (nsl, nrl)
            src = n4.at[h] if k == 1 else src.at[k - 2, h]
            dst = dst.at[k - 1, h]
        ss, rs = (sdr, rdr) if sign > 0 else (sdl, rdl)
        return rcopy(src, dst, ss.at[i], rs.at[i], dev(dz=sign * (2 if k == 1 else 1)))

    def hop_near(sign, k, h):
        zz = zr(sign * (5 - k))
        v = tacc[h, zz, near]
        if h == 1:
            v = v + fxr[1, zz].astype(F32)
        got = nrr if sign > 0 else nrl
        if k > 2:
            sums(sign, k - 1, h).wait_recv()
            v = v + got[k - 2, h].astype(F32)
        if k == 3 and h == (0 if sign > 0 else 1):
            sums(sign, 1, h).wait_recv()
            v = v + got[0, h].astype(F32)
        (nsr if sign > 0 else nsl)[k - 2, h] = v.astype(BF)
        sums(sign, k, h).start()

    def hop_far(sign, k):
        zz = zr(sign * (5 - k))
        v = tacc[0, zz, far]
        if k > 2:
            sums(sign, k - 1, 0, True).wait_recv()
            v = v + (frr if sign > 0 else frl)[k - 3].astype(F32)
        (fsr if sign > 0 else fsl)[k - 2] = v.astype(BF)
        sums(sign, k, 0, True).start()

    def begin(sign, h):
        dx(h, 4).wait_recv()
        n4[h] = (tacc[h, z4, near] + fxr[h, z4].astype(F32)).astype(BF)
        sums(sign, 1, h).start()

    BOTH = (1, -1)
    e_stage2()
    for i in (3, 5, 6, 4, 1, 2, 0):
        c1(0, i).wait_recv()
        c2(0, i).start()
    for d in (4, 3, 5):
        half_t(0, zr(d))
    for i in range(8):
        c2(0, i).wait_recv()
    full_t(0, z4)
    send_x(0, 4)
    for sign in BOTH:
        full_t(0, zr(3 * sign))
        hop_near(sign, 2, 0)
        hop_far(sign, 2)
    for i in (3, 5, 6, 4, 1, 2, 0):
        c1(1, i).wait_recv()
        c2(1, i).start()
    for sign in BOTH:
        rest(0, zr(2 * sign))
    for i in range(8):
        c2(1, i).wait_recv()
    for d in (4, 3, 5):
        rest(1, zr(d))
        send_x(1, d)
    begin(1, 0)
    e_stage3()
    for sign in BOTH:
        hop_far(sign, 3)
        rest(1, zr(2 * sign))
        send_x(1, 2 if sign > 0 else 6)
    begin(-1, 1)
    dx(1, 3).wait_recv()
    hop_near(1, 2, 1)
    dx(1, 5).wait_recv()
    hop_near(-1, 2, 1)
    for sign in BOTH:
        rest(0, zr(sign))
    hop_near(-1, 3, 0)
    hop_near(1, 3, 0)
    for sign in BOTH:
        hop_far(sign, 4)
        rest(1, zr(sign))
        send_x(1, 1 if sign > 0 else 7)
    for h in range(2):
        rest(h, z)
    send_x(1, 0)
    e_stage4()
    dx(1, 2).wait_recv()
    hop_near(1, 3, 1)
    dx(1, 6).wait_recv()
    hop_near(-1, 3, 1)
    for sign in BOTH:
        hop_near(sign, 4, 0)
    fin = rcopy(xsend, xrecv, sdx.at[9], rdx.at[9], dev(dxh=1))
    for sign in BOTH:
        sums(sign, 4, 0, True).wait_recv()
    xsend[...] = (tacc[0, z, far] + frr[2].astype(F32) + frl[2].astype(F32)).astype(BF)
    fin.start()
    e_stage5()
    dx(1, 1).wait_recv()
    hop_near(1, 4, 1)
    dx(1, 7).wait_recv()
    hop_near(-1, 4, 1)
    for sign in BOTH:
        sums(sign, 4, 0).wait_recv()
    fin.wait_recv()
    mg0 = tacc[0, z, near] + nrr[3, 0].astype(F32) + nrl[3, 0].astype(F32) + xrecv[...].astype(F32)
    res = pw[...] + dot_t(mg0.astype(BF), wm[:, pl.ds(0, H)])
    dx(1, 0).wait_recv()
    for sign in BOTH:
        sums(sign, 4, 1).wait_recv()
    mg1 = tacc[1, z, near] + nrr[3, 1].astype(F32) + nrl[3, 1].astype(F32) + fxr[1, z].astype(F32)
    outs[1] = (res + dot_t(mg1.astype(BF), wm[:, pl.ds(H, H)])).astype(BF)
    e_stage6()
    gw_out[c] = eg[...]
    e_last.wait_recv()
    gw_out[1 - c] = eg2[...]

    for ch in range(2):
        ax(ch).wait_send()
    for sign in (1, -1):
        for d in range(1, 5):
            for ch in range(2):
                if d < 4 or ch == (0 if sign > 0 else 1):
                    ring(sign, 0, d, ch).wait_send()
            across(sign, d).wait_send()
        for d in range(1, 4):
            ring(sign, 1, d, 0).wait_send()
    q1.wait_send()
    for i in range(7):
        q2(i).wait_send()
    for h in range(2):
        for p in range(2):
            b1(h, p)[1].wait_send()
        for i in range(7):
            b2(h, i).wait_send()
            c1(h, i).wait_send()
        for i in range(8):
            c2(h, i).wait_send()
    dx(0, 4).wait_send()
    for i in range(8):
        dx(1, i).wait_send()
    for sign in BOTH:
        for k in range(1, 5):
            for h in range(2):
                if k > 1 or h == (0 if sign > 0 else 1):
                    sums(sign, k, h).wait_send()
            if k > 1:
                sums(sign, k, 0, True).wait_send()
    fin.wait_send()
    e_core.wait_send()

    def sent(r, carry):
        e_xy(r).wait_send()
        e_ag(r).wait_send()
        return carry

    lax.fori_loop(1, 16, sent, 0)
    for d in range(1, 8):
        e_z(d).wait_send()
        e_back(d).wait_send()
    e_last.wait_send()


def finish(rows, gw, lo_out, gx_out, gm_out, gs_out):
    lo_out[...] = rows[0]
    gx_out[...] = rows[1]
    for m, out in enumerate((gs_out, gm_out)):
        for p in range(16):
            for d in range(8):
                rows, cols = pl.ds(d * 64 + p // 4 * 16, 16), pl.ds(p % 4 * TB, TB)
                out[rows, cols] = gw[m, p, d].astype(F32)


def shards(features, w_msg, w_self, block_index, block_count, blocks, cotangent):
    any_, smem, vmem = (pl.BlockSpec(memory_space=s) for s in (pl.ANY, pltpu.SMEM, pltpu.VMEM))
    V, D = pltpu.VMEM, pltpu.SemaphoreType.DMA
    scratch = [
        V((2, 16, TB, H), BF),
        V((F, TB), BF),
        V((8, 2, 1024, 256), BF),
        V((8, 256, 2048), BF),
        V((T, K, TB, TB), BF),
        V((T, K, TB, TB), BF),
        V((2, 2, 1024, H), F32),
        V((2, 8, 256, H), F32),
        V((F, F), BF),
        V((F, F), BF),
        V((TB, F), BF),
        V((TB, F), F32),
        V((2, 8, 8, TB), F32),
        V((8, 8, TB), F32),
        V((8, 8, TB), F32),
        V((7, 8, TB), F32),
        V((2, 1024, H), BF),
        V((2, 1024, H), BF),
        V((2, 7, TB, H), BF),
        V((2, 7, TB, H), BF),
        V((2, 2, 8, TB, H), BF),
        V((TB, F), BF),
        V((TB, F), F32),
        V((2, 8, TB, H), BF),
        V((2, 8, TB, H), BF),
        V((2, TB, H), BF),
        V((3, 2, TB, H), BF),
        V((3, 2, TB, H), BF),
        V((4, 2, TB, H), BF),
        V((4, 2, TB, H), BF),
        V((3, TB, H), BF),
        V((3, TB, H), BF),
        V((3, TB, H), BF),
        V((3, TB, H), BF),
        V((TB, H), BF),
        V((TB, H), BF),
        V((2, F, F), F32),
        V((F, F), F32),
        V((64, F), F32),
        V((8, 64, F), BF),
        V((8, 64, F), BF),
        V((16, 16, TB), F32),
        V((16, 16, TB), BF),
        V((16, 16, TB), BF),
        V((8, 16, TB), BF),
        V((16, 8, 16, TB), BF),
        V((16, 8, 16, TB), BF),
        D((6,)),
        D((10,)), D((10,)),
        D((11,)), D((11,)), D((11,)), D((11,)),
        D((8,)), D((8,)),
        D((4,)), D((4,)), D((14,)), D((14,)),
        D((14,)), D((14,)), D((16,)), D((16,)),
        D((11,)), D((11,)), D((11,)), D((11,)),
        D((10,)), D((10,)),
        D((1,)), D((1,)), D((16,)), D((16,)), D((15,)), D((15,)),
        D((16,)), D((16,)), D((1,)), D((1,)),
    ]
    parts = pl.pallas_call(
        kernel,
        out_shape=(
            jax.ShapeDtypeStruct((2, TB, F), BF),
            jax.ShapeDtypeStruct((2, 16, 8, 16, TB), BF),
        ),
        in_specs=[any_, any_, any_, smem, smem, any_, any_],
        out_specs=(vmem, vmem),
        scratch_shapes=scratch,
        compiler_params=pltpu.CompilerParams(
            collective_id=0, has_side_effects=True, vmem_limit_bytes=54 * 1024 * 1024
        ),
        name="layer",
    )(
        features,
        w_msg,
        w_self,
        block_index.reshape(T, K).T,
        block_count.reshape(T),
        blocks.reshape(T, K, TB, TB),
        cotangent,
    )
    return pl.pallas_call(
        finish,
        out_shape=(
            jax.ShapeDtypeStruct((TB, F), BF),
            jax.ShapeDtypeStruct((TB, F), BF),
            jax.ShapeDtypeStruct((F, F), F32),
            jax.ShapeDtypeStruct((F, F), F32),
        ),
        in_specs=[vmem] * 2,
        out_specs=(vmem,) * 4,
        compiler_params=pltpu.CompilerParams(vmem_limit_bytes=58 * 1024 * 1024),
        name="finish",
    )(*parts)


def solution(mesh):
    return jax.shard_map(
        shards,
        mesh=mesh,
        in_specs=(
            P(("blk", "wide"), None),
            P(),
            P(),
            P("blk", "wide", None, None),
            P("blk", "wide", None),
            P("blk", "wide", None, None, None, None),
            P(("blk", "wide"), None),
        ),
        out_specs=(P(("blk", "wide"), None), P(("blk", "wide"), None), P(), P()),
        check_vma=False,
    )
```

```python
import functools

import jax
import jax.numpy as jnp
from jax import lax
from jax.experimental import pallas as pl
from jax.experimental.pallas import tpu as pltpu
from jax.sharding import PartitionSpec as P

MESH = pl.DeviceIdType.MESH
BF = jnp.bfloat16
F32 = jnp.float32
NZ, NXH, NXL, NY, NC = 8, 2, 2, 4, 2
TB, F, H, K, T = 128, 512, 256, 4, 16
XY_PEERS = [(dxl, dy) for dxl in (1, 0) for dy in (2, 1, 3, 0) if (dxl, dy) != (0, 0)]


def dot(a, b):
    return jnp.dot(a, b, preferred_element_type=F32)


def dot_t(a, b):
    return lax.dot_general(a, b, (((1,), (1,)), ((), ())), preferred_element_type=F32)


def kernel(
    feat, w_msg_h, w_self_h, idx, cnt, blk_h, cot_h,
    outs, gw_out,
    xall, lhs, dmat, dtm, blkv, blkt, acc, tacc, wm, ws, ct, xs_self,
    sqs, sqr, sq2, sqin, b1s, b1r, b2s, b2r, g, rhs, pw,
    fxs, fxr, n4, nsr, nsl, nrr, nrl, fsr, fsl, frr, frl, xsend, xrecv,
    mats, ecr, ehalf, ezs, ezr, epc, exs, exr, ezt, eg, eg2,
    lsem, sx, rx, sr, rr, sl, rl, ssq, rsq, sb1, rb1, sb2, rb2, sc, rc_, sg, rg,
    sdr, rdr, sdl, rdl, sdx, rdx, sec, rec, sex, rex, sez, rez, sea, rea, seb, reb,
):
    bi = lax.axis_index("blk")
    wi = lax.axis_index("wide")
    z, xh = lax.div(bi, 2), lax.rem(bi, 2)
    xl, y, c = lax.div(wi, 8), lax.rem(lax.div(wi, 2), 4), lax.rem(wi, 2)
    zr = lambda d: lax.rem(z + (d + 8), 8)
    qme = xl * 4 + y

    def dev(dz=0, dxh=0, dxl=0, dy=0, dc=0):
        return (
            zr(dz) * 2 + lax.rem(xh + dxh, 2),
            lax.rem(xl + dxl, 2) * 8 + lax.rem(y + (dy + 4), 4) * 2 + lax.rem(c + dc, 2),
        )

    def rcopy(src, dst, ss, rs, device):
        return pltpu.make_async_remote_copy(
            src_ref=src, dst_ref=dst, send_sem=ss, recv_sem=rs, device_id=device, device_id_type=MESH
        )

    def plane(r):
        return dict(dxh=lax.div(r, 8), dxl=lax.rem(lax.div(r, 4), 2), dy=lax.rem(r, 4))

    def piece(r):
        o = plane(r)
        return (
            lax.rem(xh + o["dxh"], 2) * 8
            + lax.rem(xl + o["dxl"], 2) * 4
            + lax.rem(y + o["dy"], 4)
        )

    barrier = pltpu.get_barrier_semaphore()

    def greet(r, carry):
        pl.semaphore_signal(barrier, inc=1, device_id=dev(**plane(r)), device_id_type=MESH)
        return carry

    lax.fori_loop(1, 16, greet, 0)
    for d in range(1, 8):
        pl.semaphore_signal(barrier, inc=1, device_id=dev(dz=d), device_id_type=MESH)
    pl.semaphore_signal(barrier, inc=1, device_id=dev(dc=1), device_id_type=MESH)

    c_feat = [
        pltpu.make_async_copy(feat.at[:, pl.ds(h * H, H)], xall.at[h, bi], lsem.at[5 * h])
        for h in range(2)
    ]
    c_blk = pltpu.make_async_copy(blk_h, blkv, lsem.at[1])
    c_wm = pltpu.make_async_copy(w_msg_h, wm, lsem.at[2])
    c_ws = pltpu.make_async_copy(w_self_h, ws, lsem.at[3])
    c_ct = pltpu.make_async_copy(cot_h, ct, lsem.at[4])
    for cp in (*c_feat, c_blk, c_wm, c_ws, c_ct):
        cp.start()
    for cp in c_feat:
        cp.wait()
    pl.semaphore_wait(barrier, 23)

    def slot(zz, q):
        return zz * 2 + (xh if q == 0 else 1 - xh)

    def ax(ch):
        ref = xall.at[ch, bi]
        return rcopy(ref, ref, sx.at[ch], rx.at[ch], dev(dxh=1))

    def ring(sign, q, d, ch):
        behind, places = (2, 2) if d == 4 else (d - 1, 1)
        ref = xall.at[ch, slot(zr(-sign * behind), q)]
        i = q * 8 + (d - 1) * 2 + ch if q == 0 else 8 + d - 1
        ss, rs = (sr, rr) if sign > 0 else (sl, rl)
        return rcopy(ref, ref, ss.at[i], rs.at[i], dev(dz=sign * places))

    def across(sign, d):
        ch = 1 if d < 4 else (0 if sign > 0 else 1)
        ref = xall.at[ch, slot(zr(-sign * d), 0)]
        i = 2 + (d - 1) * 2 + (0 if sign > 0 else 1)
        return rcopy(ref, ref, sx.at[i], rx.at[i], dev(dxh=1))

    for ch in range(2):
        ring(1, 0, 1, ch).start()
        ring(-1, 0, 1, ch).start()
        ax(ch).start()

    def tile_of(r):
        return 2 * lax.rem(r, 8) + lax.rem(c + 1 + lax.div(r, 8), 2)

    def prepare(r, carry):
        t = tile_of(r)
        n = cnt[t]
        total = jnp.zeros((TB, TB), F32)
        for k in range(K):
            v = blkv[t, k].T
            blkt[t, k] = v
            vf = v.astype(F32)
            total += jnp.where(jnp.full((TB, TB), n, jnp.int32) > k, vf * vf, 0.0)
        row = jnp.sum(total, axis=0, keepdims=True)
        sqs[lax.div(r, 8), lax.rem(r, 8)] = jnp.broadcast_to(row, (8, TB))
        return carry

    c_blk.wait()
    lax.fori_loop(0, 8, prepare, 0)
    q1 = rcopy(sqs.at[0], sqr, ssq.at[0], rsq.at[0], dev(dc=1))
    q1.start()
    ax(0).wait_recv()
    ring(1, 1, 1, 0).start()
    ring(-1, 1, 1, 0).start()
    lax.fori_loop(8, 16, prepare, 0)

    def densify(zz):
        def row(r, carry):
            t = tile_of(r)
            rel, q = lax.div(r, 8), lax.rem(r, 8)
            n = cnt[t]
            for xs in range(2):
                s = 2 * zz + xs
                kk = jnp.int32(0)
                live = jnp.int32(0)
                for k in range(K):
                    hit = jnp.logical_and(idx[k, t] == s, k < n)
                    kk = jnp.where(hit, k, kk)
                    live = jnp.where(hit, 1, live)
                m = jnp.full((TB, TB), live, jnp.int32) > 0
                v = blkv[t, kk].astype(F32)
                vt = blkt[t, kk].astype(F32)
                dmat[zz, rel, pl.ds(pl.multiple_of(q * TB, TB), TB), pl.ds(xs * TB, TB)] = jnp.where(
                    m, v, 0.0
                ).astype(BF)
                dtm[zz, pl.ds(xs * TB, TB), pl.ds(pl.multiple_of(r * TB, TB), TB)] = jnp.where(
                    m, vt, 0.0
                ).astype(BF)
            return carry

        lax.fori_loop(0, 16, row, 0)

    def panel(zz, h):
        return xall[h, pl.ds(2 * zz, 2)].reshape(2 * TB, H)

    def pair(zz, first=False):
        densify(zz)
        for h in range(2):
            xp = panel(zz, h)
            for rel in range(2):
                for part in range(2):
                    rows = pl.ds(part * 512, 512)
                    new = dot(dmat[zz, rel, rows], xp)
                    acc[h, rel, rows] = new if first else acc[h, rel, rows] + new

    def pairs(d):
        def one(j, carry):
            pair(lax.rem(z + 8 + (2 * j - 1) * d, 8))
            return carry

        lax.fori_loop(0, 2, one, 0)

    def forward(d):
        for sign in (1, -1):
            for ch in range(2):
                ring(sign, 0, d, ch).wait_recv()
                if d < 3:
                    ring(sign, 0, d + 1, ch).start()
                if d == 2 and ch == (0 if sign > 0 else 1):
                    ring(sign, 0, 4, ch).start()
                if ch == 1:
                    across(sign, d).start()
        for sign in (1, -1):
            ring(sign, 1, d, 0).wait_recv()
            if d < 3:
                ring(sign, 1, d + 1, 0).start()

    def q_of(dxl, dy):
        return lax.rem(xl + dxl, 2) * 4 + lax.rem(y + dy, 4)

    def q2(i):
        dxl, dy = XY_PEERS[i]
        return rcopy(sq2.at[q_of(dxl, dy)], sqin.at[i], ssq.at[1 + i], rsq.at[1 + i], dev(dxl=dxl, dy=dy))

    forward(1)
    ax(1).wait_recv()
    pair(z, first=True)
    q1.wait_recv()
    sq2[...] = sqs[1] + sqr[...]
    for i in range(7):
        q2(i).start()
    forward(2)
    for sign in (1, -1):
        across(sign, 1).wait_recv()
    pairs(1)
    forward(3)
    for sign in (1, -1):
        across(sign, 2).wait_recv()
    pairs(2)
    c_ws.wait()
    xs_self[...] = dot(xall[0, bi], ws[pl.ds(0, H)]) + dot(xall[1, bi], ws[pl.ds(H, H)])
    for h in range(2):
        lhs[0, pl.ds(h * H, H)] = xall[h, bi].T
    for sign in (1, -1):
        ring(sign, 0, 4, 0 if sign > 0 else 1).wait_recv()
        across(sign, 4).start()
    for sign in (1, -1):
        across(sign, 3).wait_recv()
    pairs(3)
    z4 = zr(4)
    densify(z4)
    c_wm.wait()
    sq = sq2[qme]
    for i in range(7):
        q2(i).wait_recv()
        sq = sq + sqin[i]
    deg = 1.0 + jnp.sqrt(jnp.broadcast_to(sq[0:1], (TB, TB)).T)
    deg = jnp.concatenate([deg] * 2, axis=1)

    def b1(h, p):
        part = pl.ds(pl.multiple_of(lax.rem(xl + 1 + p, 2) * 512, 512), 512)
        i = 2 * h + p
        return part, rcopy(b1s.at[h, part], b1r.at[h, part], sb1.at[i], rb1.at[i], dev(dc=1))

    def b2(h, i):
        dxl, dy = XY_PEERS[i]
        j = 7 * h + i
        return rcopy(b2s.at[h, i], b2r.at[h, i], sb2.at[j], rb2.at[j], dev(dxl=dxl, dy=dy))

    def rows_of(q):
        return pl.ds(pl.multiple_of(q * TB, TB), TB)

    for h in range(2):
        across(1 if h == 0 else -1, 4).wait_recv()
        xp4 = panel(z4, h)
        for p in range(2):
            part, cp = b1(h, p)
            b1s[h, part] = (acc[h, 0, part] + dot(dmat[z4, 0, part], xp4)).astype(BF)
            cp.start()
        for p in range(2):
            part, cp = b1(h, p)
            acc[h, 1, part] += dot(dmat[z4, 1, part], xp4)
        for p in range(2):
            b1(h, p)[1].wait_recv()
            for i, (dxl, dy) in enumerate(XY_PEERS):
                if dxl == 1 - p:
                    rows = rows_of(q_of(dxl, dy))
                    b2s[h, i] = (acc[h, 1, rows] + b1r[h, rows].astype(F32)).astype(BF)
                    b2(h, i).start()
    c_ct.wait()
    agg = []
    for h in range(2):
        total = acc[h, 1, rows_of(qme)] + b1r[h, rows_of(qme)].astype(F32)
        for i in range(7):
            b2(h, i).wait_recv()
            total = total + b2r[h, i].astype(F32)
        agg.append(total)

    aggh = [v.astype(BF) for v in agg]
    aggl = [(v - hi.astype(F32)).astype(BF) for v, hi in zip(agg, aggh)]

    def c1(h, i):
        dxl, dy = XY_PEERS[i]
        ref = g.at[h, 1, qme]
        j = 7 * h + i
        return rcopy(ref, ref, sc.at[j], rc_.at[j], dev(dxl=dxl, dy=dy))

    def c2(h, i):
        if i == 7:
            q = qme
        else:
            dxl, dy = XY_PEERS[i]
            q = q_of(dxl, 4 - dy)
        j = 8 * h + i
        return rcopy(g.at[h, 1, q], g.at[h, 0, q], sg.at[j], rg.at[j], dev(dc=1))

    for h in range(2):
        cols = pl.ds(h * H, H)
        lin = xs_self[:, cols]
        new = sum(
            dot(v[f], wm[pl.ds(f * H, H), cols]) for v in (aggh, aggl) for f in range(2)
        )
        pre = new / deg + lin
        sig = jax.nn.sigmoid(pre)
        outs[0, :, cols] = (xall[h, bi].astype(F32) + pre * sig).astype(BF)
        ctf = ct[:, cols].astype(F32)
        pg = (ctf * sig * (1.0 + pre * (1.0 - sig))).astype(BF)
        rhs[0, :, cols] = pg
        ag = (pg.astype(F32) / deg).astype(BF)
        g[h, 1, qme] = ag
        rhs[1, :, cols] = ag
        for i in range(7):
            c1(h, i).start()
        c2(h, 7).start()

    e_core = rcopy(mats.at[1 - c], ecr, sec.at[0], rec.at[0], dev(dc=1))

    def e_last(r):
        o = plane(r)
        p = (
            lax.rem(xh + o["dxh"], 2) * 8
            + lax.rem(xl + o["dxl"], 2) * 4
            + lax.rem(y + 4 - o["dy"], 4)
        )
        return rcopy(eg.at[p], eg2.at[p], seb.at[r], reb.at[r], dev(dc=1))

    def e_z(d):
        return rcopy(ezs.at[d], ezr.at[d], sez.at[d], rez.at[d], dev(dz=d))

    def e_xy(r):
        return rcopy(exs.at[r], exr.at[r], sex.at[r], rex.at[r], dev(**plane(r)))

    def e_back(d):
        return rcopy(ezt.at[z], ezt.at[z], sez.at[7 + d], rez.at[7 + d], dev(dz=d))

    def e_ag(r):
        ref = eg.at[piece(0)]
        return rcopy(ref, ref, sea.at[r], rea.at[r], dev(**plane(r)))

    def e_stage2():
        e_core.wait_recv()
        for d in (4, 3, 5, 2, 6, 1, 7, 0):
            rows = pl.ds(pl.multiple_of(zr(d) * 64, 64), 64)
            v = mats[c, rows] + ecr[rows]
            if d:
                ezs[d] = v.astype(BF)
                e_z(d).start()
            else:
                ehalf[...] = v

    def e_stage3():
        v = ehalf[...]
        for d in range(1, 8):
            e_z(d).wait_recv()
            v = v + ezr[d].astype(F32)
        for p in range(16):
            epc[p] = v[p // 4 * 16 : p // 4 * 16 + 16, p % 4 * TB : p % 4 * TB + TB]

        def send(r, carry):
            exs[r] = epc[piece(r)].astype(BF)
            e_xy(r).start()
            return carry

        lax.fori_loop(1, 16, send, 0)

    def e_stage4():
        def take(r, total):
            e_xy(r).wait_recv()
            return total + exr[r].astype(F32)

        ezt[z] = lax.fori_loop(1, 16, take, epc[piece(0)]).astype(BF)
        for d in range(1, 8):
            e_back(d).start()

    def e_stage5():
        for d in range(1, 8):
            e_back(d).wait_recv()
        eg[piece(0)] = ezt[...]

        def send(r, carry):
            e_ag(r).start()
            return carry

        lax.fori_loop(1, 16, send, 0)
        e_last(0).start()

    def e_stage6():
        def take(r, carry):
            e_ag(r).wait_recv()
            e_last(r).start()
            return carry

        lax.fori_loop(1, 16, take, 0)

    for f in range(2):
        lhs[1, pl.ds(f * H, H)] = aggh[f].T
    mats[1 - c] = dot(lhs[1 - c], rhs[1 - c])
    e_core.start()
    mats[c] = dot(lhs[c], rhs[c])
    pw[...] = ct[...].astype(F32) + dot_t(rhs[0], ws[...])

    def half_t(h, zz):
        tacc[h, zz] = dot(dtm[zz, :, pl.ds(1024, 1024)], g[h, 1].reshape(1024, H))

    def full_t(h, zz):
        tacc[h, zz] += dot(dtm[zz, :, pl.ds(0, 1024)], g[h, 0].reshape(1024, H))

    def rest(h, zz):
        half_t(h, zz)
        full_t(h, zz)

    near = pl.ds(pl.multiple_of(xh * TB, TB), TB)
    far = pl.ds(pl.multiple_of((1 - xh) * TB, TB), TB)

    def dx(h, d):
        ref_s, ref_r = fxs.at[h, zr(d)], fxr.at[h, zr(d)]
        i = d % 8 if h == 1 else 8
        return rcopy(ref_s, ref_r, sdx.at[i], rdx.at[i], dev(dxh=1))

    def send_x(h, d):
        fxs[h, zr(d)] = tacc[h, zr(d), far].astype(BF)
        dx(h, d).start()

    def sums(sign, k, h, is_far=False):
        if is_far:
            i = 8 + k - 2
            src, dst = (fsr, frr) if sign > 0 else (fsl, frl)
            src, dst = src.at[k - 2], dst.at[k - 2]
        else:
            i = (k - 1) * 2 + h
            src, dst = (nsr, nrr) if sign > 0 else (nsl, nrl)
            src = n4.at[h] if k == 1 else src.at[k - 2, h]
            dst = dst.at[k - 1, h]
        ss, rs = (sdr, rdr) if sign > 0 else (sdl, rdl)
        return rcopy(src, dst, ss.at[i], rs.at[i], dev(dz=sign * (2 if k == 1 else 1)))

    def hop_near(sign, k, h):
        zz = zr(sign * (5 - k))
        v = tacc[h, zz, near]
        if h == 1:
            v = v + fxr[1, zz].astype(F32)
        got = nrr if sign > 0 else nrl
        if k > 2:
            sums(sign, k - 1, h).wait_recv()
            v = v + got[k - 2, h].astype(F32)
        if k == 3 and h == (0 if sign > 0 else 1):
            sums(sign, 1, h).wait_recv()
            v = v + got[0, h].astype(F32)
        (nsr if sign > 0 else nsl)[k - 2, h] = v.astype(BF)
        sums(sign, k, h).start()

    def hop_far(sign, k):
        zz = zr(sign * (5 - k))
        v = tacc[0, zz, far]
        if k > 2:
            sums(sign, k - 1, 0, True).wait_recv()
            v = v + (frr if sign > 0 else frl)[k - 3].astype(F32)
        (fsr if sign > 0 else fsl)[k - 2] = v.astype(BF)
        sums(sign, k, 0, True).start()

    def begin(sign, h):
        dx(h, 4).wait_recv()
        n4[h] = (tacc[h, z4, near] + fxr[h, z4].astype(F32)).astype(BF)
        sums(sign, 1, h).start()

    BOTH = (1, -1)
    e_stage2()
    for i in (3, 5, 6, 4, 1, 2, 0):
        c1(0, i).wait_recv()
        c2(0, i).start()
    for d in (4, 3, 5):
        half_t(0, zr(d))
    for i in range(8):
        c2(0, i).wait_recv()
    full_t(0, z4)
    send_x(0, 4)
    for sign in BOTH:
        full_t(0, zr(3 * sign))
        hop_near(sign, 2, 0)
        hop_far(sign, 2)
    for i in (3, 5, 6, 4, 1, 2, 0):
        c1(1, i).wait_recv()
        c2(1, i).start()
    for sign in BOTH:
        rest(0, zr(2 * sign))
    for i in range(8):
        c2(1, i).wait_recv()
    for d in (4, 3, 5):
        rest(1, zr(d))
        send_x(1, d)
    begin(1, 0)
    e_stage3()
    for sign in BOTH:
        hop_far(sign, 3)
        rest(1, zr(2 * sign))
        send_x(1, 2 if sign > 0 else 6)
    begin(-1, 1)
    dx(1, 3).wait_recv()
    hop_near(1, 2, 1)
    dx(1, 5).wait_recv()
    hop_near(-1, 2, 1)
    for sign in BOTH:
        rest(0, zr(sign))
    hop_near(-1, 3, 0)
    hop_near(1, 3, 0)
    e_stage4()
    for sign in BOTH:
        hop_far(sign, 4)
        rest(1, zr(sign))
        send_x(1, 1 if sign > 0 else 7)
    for h in range(2):
        rest(h, z)
    send_x(1, 0)
    dx(1, 2).wait_recv()
    hop_near(1, 3, 1)
    dx(1, 6).wait_recv()
    hop_near(-1, 3, 1)
    e_stage5()
    for sign in BOTH:
        hop_near(sign, 4, 0)
    fin = rcopy(xsend, xrecv, sdx.at[9], rdx.at[9], dev(dxh=1))
    for sign in BOTH:
        sums(sign, 4, 0, True).wait_recv()
    xsend[...] = (tacc[0, z, far] + frr[2].astype(F32) + frl[2].astype(F32)).astype(BF)
    fin.start()
    dx(1, 1).wait_recv()
    hop_near(1, 4, 1)
    dx(1, 7).wait_recv()
    hop_near(-1, 4, 1)
    for sign in BOTH:
        sums(sign, 4, 0).wait_recv()
    fin.wait_recv()
    mg0 = tacc[0, z, near] + nrr[3, 0].astype(F32) + nrl[3, 0].astype(F32) + xrecv[...].astype(F32)
    res = pw[...] + dot_t(mg0.astype(BF), wm[:, pl.ds(0, H)])
    dx(1, 0).wait_recv()
    for sign in BOTH:
        sums(sign, 4, 1).wait_recv()
    mg1 = tacc[1, z, near] + nrr[3, 1].astype(F32) + nrl[3, 1].astype(F32) + fxr[1, z].astype(F32)
    outs[1] = (res + dot_t(mg1.astype(BF), wm[:, pl.ds(H, H)])).astype(BF)
    e_stage6()
    gw_out[c] = eg[...]

    def last(r, carry):
        e_last(r).wait_recv()
        return carry

    lax.fori_loop(0, 16, last, 0)
    gw_out[1 - c] = eg2[...]

    for ch in range(2):
        ax(ch).wait_send()
    for sign in (1, -1):
        for d in range(1, 5):
            for ch in range(2):
                if d < 4 or ch == (0 if sign > 0 else 1):
                    ring(sign, 0, d, ch).wait_send()
            across(sign, d).wait_send()
        for d in range(1, 4):
            ring(sign, 1, d, 0).wait_send()
    q1.wait_send()
    for i in range(7):
        q2(i).wait_send()
    for h in range(2):
        for p in range(2):
            b1(h, p)[1].wait_send()
        for i in range(7):
            b2(h, i).wait_send()
            c1(h, i).wait_send()
        for i in range(8):
            c2(h, i).wait_send()
    dx(0, 4).wait_send()
    for i in range(8):
        dx(1, i).wait_send()
    for sign in BOTH:
        for k in range(1, 5):
            for h in range(2):
                if k > 1 or h == (0 if sign > 0 else 1):
                    sums(sign, k, h).wait_send()
            if k > 1:
                sums(sign, k, 0, True).wait_send()
    fin.wait_send()
    e_core.wait_send()

    def sent(r, carry):
        e_xy(r).wait_send()
        e_ag(r).wait_send()
        e_last(r).wait_send()
        return carry

    lax.fori_loop(1, 16, sent, 0)
    for d in range(1, 8):
        e_z(d).wait_send()
        e_back(d).wait_send()
    e_last(0).wait_send()


def finish(rows, gw, lo_out, gx_out, gm_out, gs_out):
    lo_out[...] = rows[0]
    gx_out[...] = rows[1]
    for m, out in enumerate((gs_out, gm_out)):
        for p in range(16):
            for d in range(8):
                rows, cols = pl.ds(d * 64 + p // 4 * 16, 16), pl.ds(p % 4 * TB, TB)
                out[rows, cols] = gw[m, p, d].astype(F32)


def shards(features, w_msg, w_self, block_index, block_count, blocks, cotangent):
    any_, smem, vmem = (pl.BlockSpec(memory_space=s) for s in (pl.ANY, pltpu.SMEM, pltpu.VMEM))
    V, D = pltpu.VMEM, pltpu.SemaphoreType.DMA
    scratch = [
        V((2, 16, TB, H), BF),
        V((2, F, TB), BF),
        V((8, 2, 1024, 256), BF),
        V((8, 256, 2048), BF),
        V((T, K, TB, TB), BF),
        V((T, K, TB, TB), BF),
        V((2, 2, 1024, H), F32),
        V((2, 8, 256, H), F32),
        V((F, F), BF),
        V((F, F), BF),
        V((TB, F), BF),
        V((TB, F), F32),
        V((2, 8, 8, TB), F32),
        V((8, 8, TB), F32),
        V((8, 8, TB), F32),
        V((7, 8, TB), F32),
        V((2, 1024, H), BF),
        V((2, 1024, H), BF),
        V((2, 7, TB, H), BF),
        V((2, 7, TB, H), BF),
        V((2, 2, 8, TB, H), BF),
        V((2, TB, F), BF),
        V((TB, F), F32),
        V((2, 8, TB, H), BF),
        V((2, 8, TB, H), BF),
        V((2, TB, H), BF),
        V((3, 2, TB, H), BF),
        V((3, 2, TB, H), BF),
        V((4, 2, TB, H), BF),
        V((4, 2, TB, H), BF),
        V((3, TB, H), BF),
        V((3, TB, H), BF),
        V((3, TB, H), BF),
        V((3, TB, H), BF),
        V((TB, H), BF),
        V((TB, H), BF),
        V((2, F, F), F32),
        V((F, F), F32),
        V((64, F), F32),
        V((8, 64, F), BF),
        V((8, 64, F), BF),
        V((16, 16, TB), F32),
        V((16, 16, TB), BF),
        V((16, 16, TB), BF),
        V((8, 16, TB), BF),
        V((16, 8, 16, TB), BF),
        V((16, 8, 16, TB), BF),
        D((6,)),
        D((10,)), D((10,)),
        D((11,)), D((11,)), D((11,)), D((11,)),
        D((8,)), D((8,)),
        D((4,)), D((4,)), D((14,)), D((14,)),
        D((14,)), D((14,)), D((16,)), D((16,)),
        D((11,)), D((11,)), D((11,)), D((11,)),
        D((10,)), D((10,)),
        D((1,)), D((1,)), D((16,)), D((16,)), D((15,)), D((15,)),
        D((16,)), D((16,)), D((16,)), D((16,)),
    ]
    parts = pl.pallas_call(
        kernel,
        out_shape=(
            jax.ShapeDtypeStruct((2, TB, F), BF),
            jax.ShapeDtypeStruct((2, 16, 8, 16, TB), BF),
        ),
        in_specs=[any_, any_, any_, smem, smem, any_, any_],
        out_specs=(vmem, vmem),
        scratch_shapes=scratch,
        compiler_params=pltpu.CompilerParams(
            collective_id=0, has_side_effects=True, vmem_limit_bytes=54 * 1024 * 1024
        ),
        name="layer",
    )(
        features,
        w_msg,
        w_self,
        block_index.reshape(T, K).T,
        block_count.reshape(T),
        blocks.reshape(T, K, TB, TB),
        cotangent,
    )
    return pl.pallas_call(
        finish,
        out_shape=(
            jax.ShapeDtypeStruct((TB, F), BF),
            jax.ShapeDtypeStruct((TB, F), BF),
            jax.ShapeDtypeStruct((F, F), F32),
            jax.ShapeDtypeStruct((F, F), F32),
        ),
        in_specs=[vmem] * 2,
        out_specs=(vmem,) * 4,
        compiler_params=pltpu.CompilerParams(vmem_limit_bytes=58 * 1024 * 1024),
        name="finish",
    )(*parts)


def solution(mesh):
    return jax.shard_map(
        shards,
        mesh=mesh,
        in_specs=(
            P(("blk", "wide"), None),
            P(),
            P(),
            P("blk", "wide", None, None),
            P("blk", "wide", None),
            P("blk", "wide", None, None, None, None),
            P(("blk", "wide"), None),
        ),
        out_specs=(P(("blk", "wide"), None), P(("blk", "wide"), None), P(), P()),
        check_vma=False,
    )
```
